256 devices in a mesh: row: 8 (over y, core), col: 32 (over z, x).
Axes of the slice: x: 4, y: 4, z: 8, core: 2. Of those that a mesh axis runs over, the one named last changes fastest.
Arguments:
- params: float32 [64, 8192], replicated, may hold values from -6 to 6
- momentum: float32 [8, 32, 64, 8192], P('row', 'col'), may hold values from -6 to 6
- gradient: float32 [8, 32, 64, 8192], P('row', 'col'), may hold values from -6 to 6
- chosen_rows: int32 [8, 32, 128, 4], P('row', 'col'), may hold values from 0 to 63, as said below
- live_counts: int32 [8, 32, 128], P('row', 'col'), may hold values from 1 to 4, as said below
- common_rows: int32 [32, 128, 8], P('col'), may hold values from 0 to 63, as said below
Outputs:
- new_params: float32 [64, 8192], replicated
- new_momentum: float32 [8, 32, 64, 8192], P('row', 'col')
The draws below stay inside these ranges and needn't reach their ends.
Inputs may be any that keep to these rules, and one draw needn't show every extreme that they name: `chosen_rows`: within one replica's block the 4 entries are distinct; entries at positions at or past the block's live count are ignored. `live_counts`: every replica has 4 live rows in some block. `common_rows`: within one group's block the 8 entries are distinct.
All inputs are finite; a program needn't handle non-finite values.
Results may differ from the reference program's by a relative error of at most 0.0003.
Values sent between devices are 32-bit elements; how exact they have to be, the bound alone decides.
A program may use at most 128 MiB of HBM per device.

```python
import math
import jax
import jax.numpy as jnp
from jax import lax

CH = 64
SPANS = 128
S = 4
Q = 8
W = 8192
N_ROW = 8
N_COL = 32


def order_table(key):
    keys = jax.random.split(jax.random.fold_in(key, 11), N_COL * SPANS)
    orders = jax.vmap(lambda single: jax.random.permutation(single, CH))(keys)
    return orders.reshape(N_COL, SPANS, CH).astype(jnp.int32)


def draw_common_rows(key, part):
    return order_table(key)[:, :, :Q]


def draw_chosen_rows(key, part):
    orders = order_table(key)
    keys = jax.random.split(jax.random.fold_in(key, 23), N_ROW * N_COL * SPANS)
    places = jax.vmap(lambda single: jax.random.permutation(single, 2 * Q)[:S])(keys)
    places = places.reshape(N_ROW, N_COL, SPANS, S).astype(jnp.int32)
    wide = jnp.broadcast_to(orders[None], (N_ROW, N_COL, SPANS, CH))
    return jnp.take_along_axis(wide, places, axis=3).astype(jnp.int32)


def draw_live_counts(key, part):
    counts = jax.random.randint(jax.random.fold_in(key, 31), (N_ROW, N_COL, SPANS), 1, S + 1)
    return counts.at[:, :, 0].set(S).astype(jnp.int32)


def block_scale(key, dims, pieces, low, top_value):
    def one(dim, shards_of):
        steps = jax.random.uniform(jax.random.fold_in(jax.random.fold_in(key, 6), dim), (shards_of,), jnp.float32, low / len(pieces), top_value / len(pieces))
        return jnp.repeat(jnp.exp(steps), dims[dim] // shards_of).reshape((-1,) + (1,) * (len(dims) - dim - 1))

    gain = one(*pieces[0])
    for cut in pieces[1:]:
        gain = gain * one(*cut)
    return gain


def centred(own_key, shape, scale, limit, cuts=(), kind=jnp.bfloat16):
    entries = scale * jax.random.normal(own_key, shape, jnp.float32)
    if cuts:
        entries = entries * block_scale(own_key, shape, cuts, -0.22, 0.18)
    return jnp.clip(entries, -limit, limit).astype(kind)


def setup_inputs(seed: int = 0) -> dict:
    key_list = jax.random.split(jax.random.key(seed), 7)
    params = centred(key_list[0], (CH, W), 1.0, 6.0, (), jnp.float32)
    momentum = centred(key_list[1], (N_ROW, N_COL, CH, W), 1.0, 6.0, ((0, 8), (1, 32)), jnp.float32)
    gradient = centred(key_list[2], (N_ROW, N_COL, CH, W), 1.0, 6.0, ((0, 8), (1, 32)), jnp.float32)
    chosen_rows = draw_chosen_rows(jax.random.fold_in(key_list[6], 71), 0)
    live_counts = draw_live_counts(jax.random.fold_in(key_list[6], 71), 0)
    common_rows = draw_common_rows(jax.random.fold_in(key_list[6], 71), 0)
    return {"params": params, "momentum": momentum, "gradient": gradient, "chosen_rows": chosen_rows, "live_counts": live_counts, "common_rows": common_rows}


decay_rate = 0.9
step_size = 0.1
highest = lax.Precision.HIGHEST

def dct_table(order):
    freq = jnp.arange(order, dtype=jnp.float32)[:, None]
    place = jnp.arange(order, dtype=jnp.float32)[None, :]
    matrix = math.sqrt(2.0 / order) * jnp.cos(math.pi * (2.0 * place + 1.0) * freq / (2.0 * order))
    return jnp.where(freq == 0.0, matrix * math.sqrt(0.5), matrix)

def block_pair(matrix):
    return jnp.kron(jnp.eye(2, dtype=jnp.float32), matrix)

def forward(field):
    matrix = dct_table(CH)
    across = jnp.dot(matrix, field, precision=highest, preferred_element_type=jnp.float32)
    shaped = across.reshape(-1, 2 * CH)
    result = jnp.dot(shaped, block_pair(matrix.T), precision=highest, preferred_element_type=jnp.float32)
    return result.reshape(field.shape)

def inverse(field):
    matrix = dct_table(CH)
    across = jnp.dot(matrix.T, field, precision=highest, preferred_element_type=jnp.float32)
    shaped = across.reshape(-1, 2 * CH)
    result = jnp.dot(shaped, block_pair(matrix), precision=highest, preferred_element_type=jnp.float32)
    return result.reshape(field.shape)

def pick_table(chosen, counts):
    table = (chosen[..., None] == jnp.arange(CH, dtype=jnp.int32)).astype(jnp.float32)
    if counts is not None:
        live = (jnp.arange(chosen.shape[-1], dtype=jnp.int32) < counts[..., None]).astype(jnp.float32)
        table = table * live[..., None]
    return table

def local_step(item):
    moment, grads, chosen, counts = item
    decayed = decay_rate * moment + grads
    spectrum = forward(decayed)
    cube = spectrum.reshape(CH, SPANS, CH)
    picked = pick_table(chosen, counts)
    values = jnp.einsum('ksf,fkg->ksg', picked, cube, precision=highest)
    sent = jnp.einsum('ksf,ksg->fkg', picked, values, precision=highest)
    residual = decayed - inverse(sent.reshape(CH, -1))
    return (residual, sent)

def reference(params, momentum, gradient, chosen_rows, live_counts, common_rows):

    def group_step(column):
        items = (momentum[:, column], gradient[:, column], chosen_rows[:, column], live_counts[:, column])
        residuals, sents = lax.map(local_step, items)
        summed = lax.optimization_barrier(jnp.sum(sents, axis=0))
        cut_table = pick_table(common_rows[column], None)
        kept = jnp.einsum('kqf,fkg->kqg', cut_table, summed, precision=highest)
        spread = jnp.einsum('kqf,kqg->fkg', cut_table, kept, precision=highest)
        return (residuals, spread)
    residuals, spreads = lax.map(group_step, jnp.arange(N_COL, dtype=jnp.int32))
    total = lax.optimization_barrier(jnp.sum(spreads, axis=0))
    new_params = params - step_size * inverse(total.reshape(CH, -1))
    new_momentum = jnp.transpose(residuals, (1, 0, 2, 3))
    return (new_params, new_momentum)
```

```python
import math

import jax
import jax.numpy as jnp
import numpy as np
from jax import lax
from jax.experimental import pallas as pl
from jax.experimental.pallas import tpu as pltpu
from jax.sharding import PartitionSpec as P

CH = 64
W = 8192
SPANS = 128
NY, NCORE, NZ, NX = 4, 2, 8, 4
PLANE = NY * NCORE * NX
OWN = W // PLANE
TILE = 1024
SUB = 256

decay_rate = 0.9
step_size = 0.1
MESH = pl.DeviceIdType.MESH
f32 = jnp.float32
bf16 = jnp.bfloat16


def dct_table(order):
    freq = np.arange(order)[:, None]
    place = np.arange(order)[None, :]
    matrix = math.sqrt(2.0 / order) * np.cos(math.pi * (2.0 * place + 1.0) * freq / (2.0 * order))
    return np.where(freq == 0, matrix * math.sqrt(0.5), matrix).astype(np.float32)


def table_parts():
    back = dct_table(CH).T
    high = back.astype(bf16)
    return high, (back - high.astype(np.float32)).astype(bf16)


def two_parts(value):
    high = value.astype(bf16)
    return high, (value - high.astype(f32)).astype(bf16)


def local_kernel(gather_ref, wanted_ref, chosen_ref, moment_ref, grad_ref, residual_ref, own_ref):
    freq = lax.broadcasted_iota(jnp.int32, (CH, 128), 0)
    hot = jnp.concatenate(
        [jnp.where(wanted_ref[0] == freq, 1.0, 0.0), jnp.where(chosen_ref[0] == freq, 1.0, 0.0)], axis=1
    ).astype(bf16)
    columns = jnp.dot(gather_ref[...], hot, preferred_element_type=f32)
    rows = columns.T.astype(bf16)
    back = columns[:, 128:].astype(bf16)
    back = jnp.concatenate([back[:64], back[:64], back[64:128]], axis=1)
    lane = lax.broadcasted_iota(jnp.int32, (8, 128), 1) < 64
    block_of_lane = lax.broadcasted_iota(jnp.int32, (32, SUB), 1) // 64
    block_of_row = lax.broadcasted_iota(jnp.int32, (32, SUB), 0) // 8
    same = block_of_lane == block_of_row
    for i in range(TILE // SUB):
        at = pl.ds(i * SUB, SUB)
        x = decay_rate * moment_ref[:, at] + grad_ref[:, at]
        xh, xl = two_parts(x)
        left = jnp.concatenate([rows[32 * i : 32 * i + 32], rows[128 + 32 * i : 160 + 32 * i]], axis=0)
        picked = jnp.dot(left, jnp.concatenate([xh, xh, xl], axis=0), preferred_element_type=f32)
        for h in range(2):
            part = picked[16 * h : 16 * h + 16, 128 * h : 128 * h + 128]
            own_ref[:, pl.ds(i * SUB + 128 * h, 128)] = jnp.where(lane, part[:8], part[8:])
        values = jnp.where(same, picked[32:], 0.0)
        vh, vl = two_parts(values)
        above = [jnp.zeros((32 * i, SUB), bf16)] if i else []
        below = [jnp.zeros((96 - 32 * i, SUB), bf16)] if i < 3 else []
        stack = jnp.concatenate(
            above + [vh] + below + above + [vl] + below + above + [vh] + below, axis=0
        )
        residual_ref[:, at] = x - jnp.dot(back, stack, preferred_element_type=f32)


def local_part(gather, wanted, chosen, moment, grads):
    tiles = W // TILE
    small = pl.BlockSpec((1, 1, 128), lambda t: (t, 0, 0))
    wide = pl.BlockSpec((CH, TILE), lambda t: (0, t))
    return pl.pallas_call(
        local_kernel,
        grid=(tiles,),
        in_specs=[pl.BlockSpec((192, CH), lambda t: (0, 0)), small, small, wide, wide],
        out_specs=[wide, pl.BlockSpec((8, TILE), lambda t: (0, t))],
        out_shape=[jax.ShapeDtypeStruct((CH, W), f32), jax.ShapeDtypeStruct((8, W), f32)],
        name="local_part",
    )(gather, wanted, chosen, moment, grads)


def exchange_kernel(
    own_ref, names_ref, inverse_ref, params_ref, out_ref,
    parts, values, names, mine,
    param_sem, name_send, name_recv, row_send, row_recv, deep_send, deep_recv,
    first_send, first_recv, second_send, second_recv, pair_send, pair_recv,
):
    r = lax.axis_index("row")
    c = lax.axis_index("col")
    z, x = c // NX, lax.rem(c, NX)
    y, core = r // NCORE, lax.rem(r, NCORE)
    m = r * NX + x

    def in_plane(index):
        return (index // NX, z * NX + lax.rem(index, NX))

    def along_x(d):
        return (r, z * NX + lax.rem(x + d, NX))

    def along_y(d):
        return (lax.rem(y + d, NY) * NCORE + core, c)

    def along_z(d):
        return (r, lax.rem(z + d, NZ) * NX + x)

    def lanes(index, size):
        return pl.ds(pl.multiple_of(index * size, size), size)

    def remote(src, dst, send, recv, device):
        return pltpu.make_async_remote_copy(
            src_ref=src, dst_ref=dst, send_sem=send, recv_sem=recv, device_id=device, device_id_type=MESH
        )

    params_in = pltpu.make_async_copy(params_ref.at[:, lanes(m, OWN)], mine, param_sem)
    params_in.start()
    barrier = pltpu.get_barrier_semaphore()

    def greet_plane(d, carry):
        pl.semaphore_signal(barrier, inc=1, device_id=in_plane(lax.rem(m + d, PLANE)), device_id_type=MESH)
        return carry

    def greet_deep(d, carry):
        pl.semaphore_signal(barrier, inc=1, device_id=along_z(d), device_id_type=MESH)
        return carry

    lax.fori_loop(1, PLANE, greet_plane, 0)
    lax.fori_loop(1, NZ, greet_deep, 0)
    names[z, x] = names_ref[:, lanes(m, 128)]
    parts[m] = own_ref[:, lanes(m, OWN)]
    pl.semaphore_wait(barrier, PLANE - 1 + NZ - 1)

    for d in range(1, NX):
        there = r * NX + lax.rem(x + d, NX)
        remote(names_ref.at[:, lanes(there, 128)], names.at[z, x], name_send.at[0], name_recv.at[0], along_x(d)).start()

    def send_part(d, carry):
        there = lax.rem(m + d, PLANE)
        remote(own_ref.at[:, lanes(there, OWN)], parts.at[m], row_send, row_recv, in_plane(there)).start()
        return carry

    lax.fori_loop(1, PLANE, send_part, 0)
    some = names.at[0, pl.ds(0, NX - 1)]
    arrived = remote(some, some, name_send.at[0], name_recv.at[0], along_x(1))
    arrived.wait_recv()

    def send_names(d, carry):
        remote(names.at[z], names.at[z], name_send.at[1], name_recv.at[1], along_z(d)).start()
        return carry

    lax.fori_loop(1, NZ, send_names, 0)
    some = parts.at[pl.ds(0, PLANE - 1)]
    rows_moved = remote(some, some, row_send, row_recv, along_x(1))
    rows_moved.wait_recv()
    for group in range(NX):
        total = parts[group]
        for other in range(1, NY * NCORE):
            total = total + parts[other * NX + group]
        values[z, group] = total

    def send_values(d, carry):
        remote(values.at[z], values.at[z], deep_send, deep_recv, along_z(d)).start()
        return carry

    lax.fori_loop(1, NZ, send_values, 0)
    some = names.at[pl.ds(0, NZ - 1)]
    names_moved = remote(some, some, name_send.at[1], name_recv.at[1], along_z(1))
    names_moved.wait_recv()
    listed = names[...].reshape(NZ * NX * 8, 128)
    lane = lax.broadcasted_iota(jnp.int32, (NZ * NX * 8, 128), 1)
    freq = lax.rem(lane, CH)
    spreads = []
    for h in range(2):
        first = jnp.broadcast_to(listed[:, 64 * h : 64 * h + 1], lane.shape)
        second = jnp.broadcast_to(listed[:, 64 * h + 32 : 64 * h + 33], lane.shape)
        hot = jnp.where(jnp.where(lane < CH, first, second) == freq, 1.0, 0.0)
        spreads.append(hot.T.astype(bf16))
    some = values.at[pl.ds(0, NZ - 1)]
    deep_moved = remote(some, some, deep_send, deep_recv, along_z(1))
    deep_moved.wait_recv()
    gathered = values[...].reshape(NZ * NX * 8, OWN)
    left = lax.broadcasted_iota(jnp.int32, (CH, 128), 1) < CH
    totals = []
    for h in range(2):
        high, low = two_parts(gathered[:, 128 * h : 128 * h + 128])
        both = jnp.dot(spreads[h], high, preferred_element_type=f32)
        both = both + jnp.dot(spreads[h], low, preferred_element_type=f32)
        totals.append(jnp.where(left, both[:CH], both[CH:]))
    high, low = two_parts(jnp.concatenate(totals, axis=1))
    update = jnp.dot(inverse_ref[...], jnp.concatenate([high, high, low], axis=0), preferred_element_type=f32)
    params_in.wait()
    out_ref[:, lanes(m, OWN)] = mine[...] - step_size * update

    started = []

    def go(copy):
        copy.start()
        started.append(copy)
        return copy

    def place(half, index):
        return out_ref.at[pl.ds(32 * half, 32), lanes(index, OWN)]

    def send(half, index, sems, slot, device):
        at = place(half, index)
        return go(remote(at, at, sems[0].at[slot], sems[1].at[slot], device))

    first = (first_send, first_recv)
    second = (second_send, second_recv)
    partner = (y * NCORE + (1 - core), c)

    def to_partner(half, index):
        at = place(half, index)
        go(remote(at, at, pair_send, pair_recv, partner))

    def at_x(d):
        return r * NX + lax.rem(x + NX - d, NX)

    def at_y(d):
        return (lax.rem(y + NY - d, NY) * NCORE + core) * NX + x

    def at_both(dy, dx):
        return (lax.rem(y + NY - dy, NY) * NCORE + core) * NX + lax.rem(x + NX - dx, NX)

    one = [send(0, m, first, d - 1, along_x(d)) for d in range(1, NX)]
    two = [send(1, m, first, 2 + d, along_y(d)) for d in range(1, NY)]
    over_y = [[None] * NX for _ in range(NY)]
    over_x = [[None] * NY for _ in range(NX)]
    for d in range(1, NY):
        over_y[d][0] = send(0, m, second, (d - 1) * NX, along_y(d))
    for d in range(1, NX):
        over_x[d][0] = send(1, m, second, 12 + (d - 1) * NY, along_x(d))
    to_partner(0, m)
    to_partner(1, m)
    for j in range(1, 4):
        one[j - 1].wait_recv()
        for d in range(1, NY):
            over_y[d][j] = send(0, at_x(j), second, (d - 1) * NX + j, along_y(d))
        to_partner(0, at_x(j))
        two[j - 1].wait_recv()
        for d in range(1, NX):
            over_x[d][j] = send(1, at_y(j), second, 12 + (d - 1) * NY + j, along_x(d))
        to_partner(1, at_y(j))
    for j in range(4):
        for d in range(1, 4):
            over_y[d][j].wait_recv()
            to_partner(0, at_both(d, j))
            over_x[d][j].wait_recv()
            to_partner(1, at_both(j, d))
    some = out_ref.at[:, pl.ds(0, W // 2)]
    remote(some, some, pair_send, pair_recv, partner).wait_recv()
    for copy in started:
        copy.wait_send()
    arrived.wait_send()
    rows_moved.wait_send()
    names_moved.wait_send()
    deep_moved.wait_send()


def exchange(own, names, inverse, params):
    vmem = pl.BlockSpec(memory_space=pltpu.VMEM)
    dma = pltpu.SemaphoreType.DMA
    return pl.pallas_call(
        exchange_kernel,
        out_shape=jax.ShapeDtypeStruct((CH, W), f32),
        in_specs=[vmem, vmem, vmem, pl.BlockSpec(memory_space=pl.ANY)],
        out_specs=vmem,
        scratch_shapes=[
            pltpu.VMEM((PLANE, 8, OWN), f32),
            pltpu.VMEM((NZ, NX, 8, OWN), f32),
            pltpu.VMEM((NZ, NX, 8, 128), jnp.int32),
            pltpu.VMEM((CH, OWN), f32),
            dma, dma((2,)), dma((2,)), dma, dma, dma, dma,
            dma((6,)), dma((6,)), dma((24,)), dma((24,)), dma, dma,
        ],
        compiler_params=pltpu.CompilerParams(collective_id=0, has_side_effects=True),
        name="exchange",
    )(own, names, inverse, params)


def body(params, momentum, gradient, chosen_rows, live_counts, common_rows):
    chosen, counts, common = chosen_rows[0, 0], live_counts[0, 0], common_rows[0]
    live = jnp.arange(chosen.shape[1], dtype=jnp.int32) < counts[:, None]
    chosen = jnp.where(live, chosen, -1)
    found = jnp.any(common[:, :, None] == chosen[:, None, :], axis=-1)
    wanted = jnp.where(found, common, -1)
    chosen = jnp.concatenate([chosen, jnp.full_like(chosen, -1)], axis=1)
    names = jnp.repeat(common.T, 32, axis=1)
    high, low = table_parts()
    gather = jnp.asarray(np.concatenate([high, low, high], axis=0))
    inverse = jnp.asarray(np.concatenate([high, low, high], axis=1))
    residual, own = local_part(
        gather, wanted.reshape(8, 1, 128), chosen.reshape(8, 1, 128), momentum[0, 0], gradient[0, 0]
    )
    new_params = exchange(own, names, inverse, params)
    return (new_params, residual[None, None])


def solution(mesh):
    placed = (
        P(),
        P("row", "col", None, None),
        P("row", "col", None, None),
        P("row", "col", None, None),
        P("row", "col", None),
        P("col", None, None),
    )
    return jax.shard_map(
        body,
        mesh=mesh,
        in_specs=placed,
        out_specs=(P(), P("row", "col", None, None)),
        check_vma=False,
    )
```

```python
import math

import jax
import jax.numpy as jnp
import numpy as np
from jax import lax
from jax.experimental import pallas as pl
from jax.experimental.pallas import tpu as pltpu
from jax.sharding import PartitionSpec as P

CH = 64
W = 8192
SPANS = 128
S = 4
Q = 8
NY, NCORE, NZ, NX = 4, 2, 8, 4
PLANE = NY * NCORE * NX
OWN = W // PLANE
TILE = 1024
TILES = W // TILE
SUB = 256
VMEM_GRANT = 67043328 - 2 * 4 * CH * W - 4096

decay_rate = 0.9
step_size = 0.1
MESH = pl.DeviceIdType.MESH
f32 = jnp.float32
bf16 = jnp.bfloat16


def dct_table(order):
    freq = np.arange(order)[:, None]
    place = np.arange(order)[None, :]
    matrix = math.sqrt(2.0 / order) * np.cos(math.pi * (2.0 * place + 1.0) * freq / (2.0 * order))
    return np.where(freq == 0, matrix * math.sqrt(0.5), matrix).astype(np.float32)


def table_parts():
    back = dct_table(CH).T
    high = back.astype(bf16)
    return high, (back - high.astype(np.float32)).astype(bf16)


def two_parts(value):
    high = value.astype(bf16)
    return high, (value - high.astype(f32)).astype(bf16)


def step_kernel(
    gather_hbm, inverse_hbm, common_hbm, chosen_hbm, counts_hbm, moment_ref, grad_ref, params_ref,
    out_ref, residual_ref,
    gather_ref, inverse_ref, common_ref, chosen_ref, counts_ref, small_sem,
    decayed, grads, hot_wanted, hot_chosen, wanted_rows, chosen_rows, chosen_values, own, parts, values, names, mine,
    moment_sem, grad_sem, param_sem, name_send, name_recv, row_send, row_recv, deep_send, deep_recv,
    first_send, first_recv, second_send, second_recv, pair_send, pair_recv,
):
    r = lax.axis_index("row")
    c = lax.axis_index("col")
    z, x = c // NX, lax.rem(c, NX)
    y, core = r // NCORE, lax.rem(r, NCORE)
    m = r * NX + x

    def in_plane(index):
        return (index // NX, z * NX + lax.rem(index, NX))

    def along_x(d):
        return (r, z * NX + lax.rem(x + d, NX))

    def along_y(d):
        return (lax.rem(y + d, NY) * NCORE + core, c)

    def along_z(d):
        return (r, lax.rem(z + d, NZ) * NX + x)

    def lanes(index, size):
        return pl.ds(pl.multiple_of(index * size, size), size)

    def half_lanes(index, h):
        return pl.ds(pl.multiple_of(index * OWN + 128 * h, 128), 128)

    def remote(src, dst, send, recv, device):
        return pltpu.make_async_remote_copy(
            src_ref=src, dst_ref=dst, send_sem=send, recv_sem=recv, device_id=device, device_id_type=MESH
        )

    def moment_in(t):
        return pltpu.make_async_copy(moment_ref.at[:, lanes(t, TILE)], decayed.at[:, lanes(t, TILE)], moment_sem.at[t])

    def grad_in(t):
        return pltpu.make_async_copy(grad_ref.at[:, lanes(t, TILE)], grads.at[:, lanes(t, TILE)], grad_sem.at[t])

    smalls = [
        pltpu.make_async_copy(src, dst, small_sem.at[i])
        for i, (src, dst) in enumerate(
            [
                (chosen_hbm, chosen_ref),
                (counts_hbm, counts_ref),
                (common_hbm, common_ref),
                (gather_hbm, gather_ref),
                (inverse_hbm, inverse_ref),
            ]
        )
    ]
    for copy in smalls:
        copy.start()
    for t in range(TILES):
        moment_in(t).start()
        grad_in(t).start()
    params_in = pltpu.make_async_copy(params_ref.at[:, lanes(m, OWN)], mine, param_sem)
    params_in.start()
    barrier = pltpu.get_barrier_semaphore()

    def greet_plane(d, carry):
        pl.semaphore_signal(barrier, inc=1, device_id=in_plane(lax.rem(m + d, PLANE)), device_id_type=MESH)
        return carry

    def greet_deep(d, carry):
        pl.semaphore_signal(barrier, inc=1, device_id=along_z(d), device_id_type=MESH)
        return carry

    lax.fori_loop(1, NZ, greet_deep, 0)
    lax.fori_loop(1, PLANE, greet_plane, 0)

    for copy in smalls:
        copy.wait()
    common = common_ref[...]
    place = lax.broadcasted_iota(jnp.int32, (S, SPANS), 0)
    chosen = jnp.where(place < counts_ref[...], chosen_ref[...], -1)
    found = common == chosen[0:1]
    for s in range(1, S):
        found = found | (common == chosen[s : s + 1])
    wanted = jnp.where(found, common, -1)
    freq = lax.broadcasted_iota(jnp.int32, (128, SPANS), 0)
    for q in range(Q):
        hot_wanted[pl.ds(q, SPANS, stride=Q), :] = jnp.where(wanted[q : q + 1] == freq, 1.0, 0.0).T
    for s in range(S):
        hot_chosen[pl.ds(s, SPANS, stride=S), :] = jnp.where(chosen[s : s + 1] == freq, 1.0, 0.0).T
    wanted_rows[...] = jnp.dot(
        hot_wanted[...].astype(bf16), gather_ref[...], preferred_element_type=f32
    ).astype(bf16)
    chosen_rows[...] = jnp.dot(hot_chosen[...].astype(bf16), gather_ref[...], preferred_element_type=f32)
    names[z, x] = common
    left_lane = lax.broadcasted_iota(jnp.int32, (8, 128), 1) < CH

    def local_sums(t, carry):
        moment_in(t).wait()
        grad_in(t).wait()
        for i in range(TILE // SUB):
            at = pl.ds(pl.multiple_of(t * TILE + i * SUB, SUB), SUB)
            field = decay_rate * decayed[:, at] + grads[:, at]
            decayed[:, at] = field
            high, low = two_parts(field)
            step = t * (TILE // SUB) + i
            left = jnp.concatenate(
                [
                    wanted_rows[pl.ds(pl.multiple_of(step * 4 * Q, 4 * Q), 4 * Q), :],
                    chosen_rows[pl.ds(pl.multiple_of(step * 4 * S, 4 * S), 4 * S), :].astype(bf16),
                ],
                axis=0,
            )
            picked = jnp.dot(left, jnp.concatenate([high, high, low], axis=0), preferred_element_type=f32)
            for h in range(2):
                part = picked[16 * h : 16 * h + 16, 128 * h : 128 * h + 128]
                own[:, pl.ds(pl.multiple_of(t * TILE + i * SUB + 128 * h, 128), 128)] = jnp.where(
                    left_lane, part[:8], part[8:]
                )
            chosen_values[:, at] = picked[4 * Q :]
        return carry

    lax.fori_loop(0, TILES, local_sums, 0)
    pl.semaphore_wait(barrier, PLANE - 1 + NZ - 1)

    for d in range(1, NX):
        remote(common_ref, names.at[z, x], name_send.at[0], name_recv.at[0], along_x(d)).start()
    for h in range(2):

        def send_part(d, carry):
            there = lax.rem(m + d, PLANE)
            remote(
                own.at[:, half_lanes(there, h)], parts.at[h, m], row_send.at[h], row_recv.at[h], in_plane(there)
            ).start()
            return carry

        lax.fori_loop(1, PLANE, send_part, 0)
        parts[h, m] = own[:, half_lanes(m, h)]
    some = names.at[0, pl.ds(0, NX - 1)]
    near_names = remote(some, some, name_send.at[0], name_recv.at[0], along_x(1))
    near_names.wait_recv()

    def send_names(d, carry):
        remote(names.at[z], names.at[z], name_send.at[1], name_recv.at[1], along_z(d)).start()
        return carry

    lax.fori_loop(1, NZ, send_names, 0)

    same = lax.broadcasted_iota(jnp.int32, (4 * S, SUB), 1) // CH == lax.broadcasted_iota(jnp.int32, (4 * S, SUB), 0) // S

    def residuals(t, carry):
        for i in range(TILE // SUB):
            at = pl.ds(pl.multiple_of(t * TILE + i * SUB, SUB), SUB)
            step = t * (TILE // SUB) + i
            rows = chosen_rows[pl.ds(pl.multiple_of(step * 4 * S, 4 * S), 4 * S), :]
            back = jnp.concatenate([rows[:, :CH], rows[:, :CH], rows[:, CH : 2 * CH]], axis=0).T.astype(bf16)
            high, low = two_parts(jnp.where(same, chosen_values[:, at], 0.0))
            sent = jnp.dot(back, jnp.concatenate([high, low, high], axis=0), preferred_element_type=f32)
            residual_ref[:, at] = decayed[:, at] - sent
        return carry

    lax.fori_loop(0, TILES, residuals, 0)

    rows_moved = []
    for h in range(2):
        some = parts.at[h, pl.ds(0, PLANE - 1)]
        moved = remote(some, some, row_send.at[h], row_recv.at[h], along_x(1))
        moved.wait_recv()
        rows_moved.append(moved)
        for group in range(NX):
            total = parts[h, group]
            for other in range(1, NY * NCORE):
                total = total + parts[h, other * NX + group]
            values[h, z, group] = total

        def send_values(d, carry):
            remote(values.at[h, z], values.at[h, z], deep_send.at[h], deep_recv.at[h], along_z(d)).start()
            return carry

        lax.fori_loop(1, NZ, send_values, 0)

    some = names.at[pl.ds(0, NZ - 1)]
    far_names = remote(some, some, name_send.at[1], name_recv.at[1], along_z(1))
    far_names.wait_recv()
    listed = names[...].reshape(NZ * NX * Q, SPANS).astype(f32).astype(bf16)
    lane = lax.broadcasted_iota(jnp.int32, (128, 128), 1)
    block = lax.broadcasted_iota(jnp.int32, (128, 128), 0)
    wide_lane = lax.broadcasted_iota(jnp.int32, (NZ * NX * Q, 128), 1)
    wide_freq = lax.rem(wide_lane, CH).astype(f32)
    spreads = []
    for h in range(2):
        pick = jnp.where(block == m * 4 + 2 * h + lane // CH, 1.0, 0.0).astype(bf16)
        spread_names = jnp.dot(listed, pick, preferred_element_type=f32)
        spreads.append(jnp.where(spread_names == wide_freq, 1.0, 0.0).T.astype(bf16))
    params_in.wait()
    left = lax.broadcasted_iota(jnp.int32, (CH, 128), 1) < CH

    started = []

    def go(copy):
        copy.start()
        started.append(copy)
        return copy

    def place_of(h, rows, index):
        return out_ref.at[pl.ds(32 * rows, 32), half_lanes(index, h)]

    def send(h, rows, index, sems, slot, device):
        at = place_of(h, rows, index)
        return go(remote(at, at, sems[0].at[h, slot], sems[1].at[h, slot], device))

    first = (first_send, first_recv)
    second = (second_send, second_recv)
    partner = (y * NCORE + (1 - core), c)

    def to_partner(h, rows, index):
        at = place_of(h, rows, index)
        go(remote(at, at, pair_send, pair_recv, partner))

    def at_x(d):
        return r * NX + lax.rem(x + NX - d, NX)

    def at_y(d):
        return (lax.rem(y + NY - d, NY) * NCORE + core) * NX + x

    def at_both(dy, dx):
        return (lax.rem(y + NY - dy, NY) * NCORE + core) * NX + lax.rem(x + NX - dx, NX)

    deep_moved = []
    over = []
    for h in range(2):
        some = values.at[h, pl.ds(0, NZ - 1)]
        moved = remote(some, some, deep_send.at[h], deep_recv.at[h], along_z(1))
        moved.wait_recv()
        deep_moved.append(moved)
        high, low = two_parts(values[h].reshape(NZ * NX * Q, 128))
        both = jnp.dot(spreads[h], high, preferred_element_type=f32)
        both = both + jnp.dot(spreads[h], low, preferred_element_type=f32)
        high, low = two_parts(jnp.where(left, both[:CH], both[CH:]))
        update = jnp.dot(inverse_ref[...], jnp.concatenate([high, high, low], axis=0), preferred_element_type=f32)
        out_ref[:, half_lanes(m, h)] = mine[:, 128 * h : 128 * h + 128] - step_size * update
        one = [send(h, 0, m, first, d - 1, along_x(d)) for d in range(1, NX)]
        two = [send(h, 1, m, first, 2 + d, along_y(d)) for d in range(1, NY)]
        over_y = [[None] * NX for _ in range(NY)]
        over_x = [[None] * NY for _ in range(NX)]
        for d in range(1, NY):
            over_y[d][0] = send(h, 0, m, second, (d - 1) * NX, along_y(d))
        for d in range(1, NX):
            over_x[d][0] = send(h, 1, m, second, 12 + (d - 1) * NY, along_x(d))
        to_partner(h, 0, m)
        to_partner(h, 1, m)
        over.append((one, two, over_y, over_x))
    for h in range(2):
        one, two, over_y, over_x = over[h]
        for j in range(1, 4):
            one[j - 1].wait_recv()
            for d in range(1, NY):
                over_y[d][j] = send(h, 0, at_x(j), second, (d - 1) * NX + j, along_y(d))
            to_partner(h, 0, at_x(j))
            two[j - 1].wait_recv()
            for d in range(1, NX):
                over_x[d][j] = send(h, 1, at_y(j), second, 12 + (d - 1) * NY + j, along_x(d))
            to_partner(h, 1, at_y(j))
    for h in range(2):
        one, two, over_y, over_x = over[h]
        for j in range(4):
            for d in range(1, 4):
                over_y[d][j].wait_recv()
                to_partner(h, 0, at_both(d, j))
                over_x[d][j].wait_recv()
                to_partner(h, 1, at_both(j, d))
    some = out_ref.at[:, pl.ds(0, W // 2)]
    remote(some, some, pair_send, pair_recv, partner).wait_recv()
    for copy in started + rows_moved + deep_moved + [near_names, far_names]:
        copy.wait_send()


def step(gather, inverse, common, chosen, counts, momentum, gradient, params):
    vmem = pl.BlockSpec(memory_space=pltpu.VMEM)
    outside = pl.BlockSpec(memory_space=pltpu.HBM)
    dma = pltpu.SemaphoreType.DMA
    return pl.pallas_call(
        step_kernel,
        out_shape=(pltpu.VMEM((CH, W), f32), pltpu.VMEM((CH, W), f32)),
        in_specs=[outside] * 8,
        out_specs=(vmem, vmem),
        scratch_shapes=[
            pltpu.VMEM((128, 3 * CH), bf16),
            pltpu.VMEM((CH, 3 * CH), bf16),
            pltpu.VMEM((Q, SPANS), jnp.int32),
            pltpu.VMEM((S, SPANS), jnp.int32),
            pltpu.VMEM((1, SPANS), jnp.int32),
            dma((5,)),
            pltpu.VMEM((CH, W), f32),
            pltpu.VMEM((CH, W), f32),
            pltpu.VMEM((SPANS * Q, 128), f32),
            pltpu.VMEM((SPANS * S, 128), f32),
            pltpu.VMEM((SPANS * Q, 3 * CH), bf16),
            pltpu.VMEM((SPANS * S, 3 * CH), f32),
            pltpu.VMEM((4 * S, W), f32),
            pltpu.VMEM((Q, W), f32),
            pltpu.VMEM((2, PLANE, Q, 128), f32),
            pltpu.VMEM((2, NZ, NX, Q, 128), f32),
            pltpu.VMEM((NZ, NX, Q, SPANS), jnp.int32),
            pltpu.VMEM((CH, OWN), f32),
            dma((TILES,)), dma((TILES,)), dma, dma((2,)), dma((2,)), dma((2,)), dma((2,)), dma((2,)), dma((2,)),
            dma((2, 6)), dma((2, 6)), dma((2, 24)), dma((2, 24)), dma, dma,
        ],
        compiler_params=pltpu.CompilerParams(collective_id=0, has_side_effects=True, vmem_limit_bytes=VMEM_GRANT),
        name="step",
    )(gather, inverse, common, chosen, counts, momentum, gradient, params)


def deliver_kernel(first_ref, second_ref, first_out, second_out, sems):
    copies = []
    for t in range(TILES):
        for i, (src, dst) in enumerate([(first_ref, first_out), (second_ref, second_out)]):
            at = pl.ds(t * TILE, TILE)
            copies.append(pltpu.make_async_copy(src.at[:, at], dst.at[:, at], sems.at[i, t]))
    for copy in copies:
        copy.start()
    for copy in copies:
        copy.wait()


def deliver(first, second):
    vmem = pl.BlockSpec(memory_space=pltpu.VMEM)
    outside = pl.BlockSpec(memory_space=pltpu.HBM)
    shape = jax.ShapeDtypeStruct((CH, W), f32)
    return pl.pallas_call(
        deliver_kernel,
        out_shape=(shape, shape),
        in_specs=[vmem, vmem],
        out_specs=(outside, outside),
        scratch_shapes=[pltpu.SemaphoreType.DMA((2, TILES))],
        compiler_params=pltpu.CompilerParams(vmem_limit_bytes=1 << 20),
        name="deliver",
    )(first, second)


def body(params, momentum, gradient, chosen_rows, live_counts, common_rows):
    high, low = table_parts()
    gather = np.concatenate([high.T, low.T, high.T], axis=1)
    gather = jnp.asarray(np.concatenate([gather, np.zeros_like(gather)], axis=0))
    inverse = jnp.asarray(np.concatenate([high, low, high], axis=1))
    new_params, residual = step(
        gather, inverse, common_rows[0].T, chosen_rows[0, 0].T, live_counts[0], momentum[0, 0], gradient[0, 0], params
    )
    new_params, residual = deliver(new_params, residual)
    return (new_params, residual[None, None])


def solution(mesh):
    placed = (
        P(),
        P("row", "col", None, None),
        P("row", "col", None, None),
        P("row", "col", None, None),
        P("row", "col", None),
        P("col", None, None),
    )
    return jax.shard_map(
        body,
        mesh=mesh,
        in_specs=placed,
        out_specs=(P(), P("row", "col", None, None)),
        check_vma=False,
    )
```

```python
import math

import jax
import jax.numpy as jnp
import numpy as np
from jax import lax
from jax.experimental import pallas as pl
from jax.experimental.pallas import tpu as pltpu
from jax.sharding import PartitionSpec as P

CH = 64
W = 8192
SPANS = 128
S = 4
Q = 8
NY, NCORE, NZ, NX = 4, 2, 8, 4
PLANE = NY * NCORE * NX
OWN = W // PLANE
TILE = 1024
TILES = W // TILE
SUB = 256
GATHER_COPIES = 2 * (2 * 3 + 2 * 12 + 2 * 16)
EARLY, LATE = (0, 1, 2), (3, 6, 4, 5, 7)
VMEM_GRANT = 67043328 - 2 * 4 * CH * W - 4096

decay_rate = 0.9
step_size = 0.1
MESH = pl.DeviceIdType.MESH
f32 = jnp.float32
bf16 = jnp.bfloat16


def dct_table(order):
    freq = np.arange(order)[:, None]
    place = np.arange(order)[None, :]
    matrix = math.sqrt(2.0 / order) * np.cos(math.pi * (2.0 * place + 1.0) * freq / (2.0 * order))
    return np.where(freq == 0, matrix * math.sqrt(0.5), matrix).astype(np.float32)


def table_parts():
    back = dct_table(CH).T
    high = back.astype(bf16)
    return high, (back - high.astype(np.float32)).astype(bf16)


def steps_by_distance():
    steps = [(dy, dk, dx) for dy in range(NY) for dk in range(NCORE) for dx in range(NX)][1:]
    return sorted(steps, key=lambda s: -(min(s[0], NY - s[0]) + min(s[2], NX - s[2])))


def two_parts(value):
    high = value.astype(bf16)
    return high, (value - high.astype(f32)).astype(bf16)


def step_kernel(
    gather_hbm, inverse_hbm, common_hbm, chosen_hbm, counts_hbm, moment_ref, grad_ref, params_ref,
    out_ref, residual_ref,
    gather_ref, inverse_ref, common_ref, chosen_ref, counts_ref, small_sem,
    decayed, grads, hot_wanted, hot_chosen, wanted_rows, chosen_rows, chosen_values, own, parts, values, near, names, mine,
    moment_sem, grad_sem, param_sem, name_send, name_recv, row_send, row_recv, deep_send, deep_recv,
    gather_send, first_recv, second_recv, pair_recv,
):
    r = lax.axis_index("row")
    c = lax.axis_index("col")
    z, x = c // NX, lax.rem(c, NX)
    y, core = r // NCORE, lax.rem(r, NCORE)
    m = r * NX + x

    def in_plane(index):
        return (index // NX, z * NX + lax.rem(index, NX))

    def shifted(dy, dk, dx):
        row = lax.rem(y + dy, NY) * NCORE + lax.rem(core + dk, NCORE)
        return row * NX + lax.rem(x + dx, NX)

    def along_x(d):
        return (r, z * NX + lax.rem(x + d, NX))

    def along_y(d):
        return (lax.rem(y + d, NY) * NCORE + core, c)

    def along_z(d):
        return (r, lax.rem(z + d, NZ) * NX + x)

    def lanes(index, size):
        return pl.ds(pl.multiple_of(index * size, size), size)

    def half_lanes(index, h):
        return pl.ds(pl.multiple_of(h * (W // 2) + 128 * index, 128), 128)

    def remote(src, dst, send, recv, device):
        return pltpu.make_async_remote_copy(
            src_ref=src, dst_ref=dst, send_sem=send, recv_sem=recv, device_id=device, device_id_type=MESH
        )

    def moment_in(t):
        return pltpu.make_async_copy(moment_ref.at[:, lanes(t, TILE)], decayed.at[:, lanes(t, TILE)], moment_sem.at[t])

    def grad_in(t):
        return pltpu.make_async_copy(grad_ref.at[:, lanes(t, TILE)], grads.at[:, lanes(t, TILE)], grad_sem.at[t])

    barrier = pltpu.get_barrier_semaphore()

    def greet_deep(d, carry):
        pl.semaphore_signal(barrier, inc=1, device_id=along_z(d), device_id_type=MESH)
        return carry

    for step in steps_by_distance():
        there = shifted(*step)
        pl.semaphore_signal(barrier, inc=1, device_id=in_plane(there), device_id_type=MESH)

    lax.fori_loop(1, NZ, greet_deep, 0)
    smalls = [
        pltpu.make_async_copy(src, dst, small_sem.at[i])
        for i, (src, dst) in enumerate(
            [
                (chosen_hbm, chosen_ref),
                (counts_hbm, counts_ref),
                (common_hbm, common_ref),
                (gather_hbm, gather_ref),
                (inverse_hbm, inverse_ref),
            ]
        )
    ]
    for copy in smalls:
        copy.start()
    for t in range(TILES // 2):
        moment_in(t).start()
        grad_in(t).start()
    params_in = [
        pltpu.make_async_copy(params_ref.at[:, half_lanes(m, h)], mine.at[h], param_sem.at[h]) for h in range(2)
    ]
    for copy in params_in:
        copy.start()
    for copy in smalls:
        copy.wait()
    common = common_ref[...]
    place = lax.broadcasted_iota(jnp.int32, (S, SPANS), 0)
    chosen = jnp.where(place < counts_ref[...], chosen_ref[...], -1)
    found = common == chosen[0:1]
    for s in range(1, S):
        found = found | (common == chosen[s : s + 1])
    wanted = jnp.where(found, common, -1)
    freq = lax.broadcasted_iota(jnp.int32, (128, SPANS), 0)
    for q in range(Q):
        hot_wanted[pl.ds(q, SPANS, stride=Q), :] = jnp.where(wanted[q : q + 1] == freq, 1.0, 0.0).T
    for s in range(S):
        hot_chosen[pl.ds(s, SPANS, stride=S), :] = jnp.where(chosen[s : s + 1] == freq, 1.0, 0.0).T
    wanted_rows[...] = jnp.dot(
        hot_wanted[...].astype(bf16), gather_ref[...], preferred_element_type=f32
    ).astype(bf16)
    chosen_rows[...] = jnp.dot(hot_chosen[...].astype(bf16), gather_ref[...], preferred_element_type=f32)
    near[x] = common.astype(f32)
    left_lane = lax.broadcasted_iota(jnp.int32, (8, 128), 1) < CH

    def local_sums(t, carry):
        moment_in(t).wait()
        grad_in(t).wait()

        @pl.when(t < TILES // 2)
        def _():
            moment_in(t + TILES // 2).start()
            grad_in(t + TILES // 2).start()

        for i in range(TILE // SUB):
            at = pl.ds(pl.multiple_of(t * TILE + i * SUB, SUB), SUB)
            field = decay_rate * decayed[:, at] + grads[:, at]
            decayed[:, at] = field
            high, low = two_parts(field)
            step = t * (TILE // SUB) + i
            left = jnp.concatenate(
                [
                    wanted_rows[pl.ds(pl.multiple_of(step * 4 * Q, 4 * Q), 4 * Q), :],
                    chosen_rows[pl.ds(pl.multiple_of(step * 4 * S, 4 * S), 4 * S), :].astype(bf16),
                ],
                axis=0,
            )
            picked = jnp.dot(left, jnp.concatenate([high, high, low], axis=0), preferred_element_type=f32)
            for h in range(2):
                part = picked[16 * h : 16 * h + 16, 128 * h : 128 * h + 128]
                own[:, pl.ds(pl.multiple_of(t * TILE + i * SUB + 128 * h, 128), 128)] = jnp.where(
                    left_lane, part[:8], part[8:]
                )
            chosen_values[:, at] = picked[4 * Q :]
        return carry

    for h in range(2):
        lax.fori_loop(h * (TILES // 2), (h + 1) * (TILES // 2), local_sums, 0)
        if h == 0:
            pl.semaphore_wait(barrier, PLANE - 1 + NZ - 1)
            for d in range(1, NX):
                remote(near.at[x], near.at[x], name_send.at[0], name_recv.at[0], along_x(d)).start()

        for step in steps_by_distance():
            there = shifted(*step)
            remote(
                own.at[:, half_lanes(there, h)], parts.at[h, m], row_send.at[h], row_recv.at[h], in_plane(there)
            ).start()
        parts[h, m] = own[:, half_lanes(m, h)]
    some = near.at[pl.ds(0, NX - 1)]
    near_names = remote(some, some, name_send.at[0], name_recv.at[0], along_x(1))
    near_names.wait_recv()
    lane = lax.broadcasted_iota(jnp.int32, (128, 128), 1)
    block = lax.broadcasted_iota(jnp.int32, (128, 128), 0)
    mine_of = m * 2 + lax.rem(lane, 2) + (SPANS // 2) * lax.rem(lane // 2, 2)
    listed = jnp.zeros((Q, 128), f32)
    for group in range(NX):
        pick = jnp.where((block == mine_of) & (lane // 4 == group), 1.0, 0.0).astype(bf16)
        listed = listed + jnp.dot(near[group].astype(bf16), pick, preferred_element_type=f32)
    names[z] = listed

    def send_names(d, carry):
        remote(names.at[z], names.at[z], name_send.at[1], name_recv.at[1], along_z(d)).start()
        return carry

    lax.fori_loop(1, NZ, send_names, 0)

    same = lax.broadcasted_iota(jnp.int32, (4 * S, SUB), 1) // CH == lax.broadcasted_iota(jnp.int32, (4 * S, SUB), 0) // S

    def residuals(t, carry):
        for i in range(TILE // SUB):
            at = pl.ds(pl.multiple_of(t * TILE + i * SUB, SUB), SUB)
            step = t * (TILE // SUB) + i
            rows = chosen_rows[pl.ds(pl.multiple_of(step * 4 * S, 4 * S), 4 * S), :]
            back = jnp.concatenate([rows[:, :CH], rows[:, :CH], rows[:, CH : 2 * CH]], axis=0).T.astype(bf16)
            high, low = two_parts(jnp.where(same, chosen_values[:, at], 0.0))
            sent = jnp.dot(back, jnp.concatenate([high, low, high], axis=0), preferred_element_type=f32)
            residual_ref[:, at] = decayed[:, at] - sent
        return carry

    lax.fori_loop(0, TILES, residuals, 0)

    def send_values(h, deep):
        @pl.when(z != deep)
        def _():
            remote(
                values.at[h, z], values.at[h, z], deep_send.at[h], deep_recv.at[h], (r, deep * NX + x)
            ).start()

    rows_moved = []
    for h in range(2):
        some = parts.at[h, pl.ds(0, PLANE - 1)]
        moved = remote(some, some, row_send.at[h], row_recv.at[h], along_x(1))
        moved.wait_recv()
        rows_moved.append(moved)
        for group in range(NX):
            total = parts[h, group]
            for other in range(1, NY * NCORE):
                total = total + parts[h, other * NX + group]
            values[h, z, group] = total
        for deep in EARLY:
            send_values(h, deep)
    for h in range(2):
        for deep in LATE:
            send_values(h, deep)

    some = names.at[pl.ds(0, NZ - 1)]
    far_names = remote(some, some, name_send.at[1], name_recv.at[1], along_z(1))
    far_names.wait_recv()
    listed = names[...].reshape(NZ * Q, 128).astype(bf16)
    wide_freq = lax.rem(lax.broadcasted_iota(jnp.int32, (NZ * NX * Q, 128), 1), CH).astype(f32)
    spreads = []
    for h in range(2):
        found_names = []
        for group in range(NX):
            pick = jnp.where(block == 4 * group + 2 * h + lane // CH, 1.0, 0.0).astype(bf16)
            found_names.append(jnp.dot(listed, pick, preferred_element_type=f32).reshape(NZ, Q, 128))
        spread_names = jnp.stack(found_names, axis=1).reshape(NZ * NX * Q, 128)
        hot = jnp.where(spread_names == wide_freq, 1.0, 0.0).T.astype(bf16)
        spreads.append(jnp.dot(inverse_ref[...], hot, preferred_element_type=f32).astype(bf16))
    for copy in params_in:
        copy.wait()
    left = lax.broadcasted_iota(jnp.int32, (CH, 128), 1) < CH

    def go(copy):
        copy.start()
        return copy

    def place_of(h, rows, index):
        return out_ref.at[pl.ds(32 * rows, 32), half_lanes(index, h)]

    def send(h, rows, index, sems, slot, device):
        at = place_of(h, rows, index)
        return go(remote(at, at, gather_send, sems.at[h, slot], device))

    partner = (y * NCORE + (1 - core), c)

    def to_partner(h, rows, index):
        at = place_of(h, rows, index)
        go(remote(at, at, gather_send, pair_recv, partner))

    def at_x(d):
        return r * NX + lax.rem(x + NX - d, NX)

    def at_y(d):
        return (lax.rem(y + NY - d, NY) * NCORE + core) * NX + x

    def at_both(dy, dx):
        return (lax.rem(y + NY - dy, NY) * NCORE + core) * NX + lax.rem(x + NX - dx, NX)

    deep_moved = []
    over = []
    for h in range(2):
        some = values.at[h, pl.ds(0, NZ - 1)]
        moved = remote(some, some, deep_send.at[h], deep_recv.at[h], along_z(1))
        moved.wait_recv()
        deep_moved.append(moved)
        high, low = two_parts(values[h].reshape(NZ * NX * Q, 128))
        both = jnp.dot(spreads[h], high, preferred_element_type=f32)
        both = both[:128] + both[128:] + jnp.dot(spreads[h][:128], low, preferred_element_type=f32)
        update = jnp.where(left, both[:CH], both[CH:])
        out_ref[:, half_lanes(m, h)] = mine[h] - step_size * update
        one = [send(h, 0, m, first_recv, d - 1, along_x(d)) for d in range(1, NX)]
        two = [send(h, 1, m, first_recv, 2 + d, along_y(d)) for d in range(1, NY)]
        over_y = [[None] * NX for _ in range(NY)]
        over_x = [[None] * NY for _ in range(NX)]
        for d in range(1, NY):
            over_y[d][0] = send(h, 0, m, second_recv, (d - 1) * NX, along_y(d))
        for d in range(1, NX):
            over_x[d][0] = send(h, 1, m, second_recv, 12 + (d - 1) * NY, along_x(d))
        to_partner(h, 0, m)
        to_partner(h, 1, m)
        over.append((one, two, over_y, over_x))
    for h in range(2):
        one, two, over_y, over_x = over[h]
        for j in range(1, 4):
            one[j - 1].wait_recv()
            for d in range(1, NY):
                over_y[d][j] = send(h, 0, at_x(j), second_recv, (d - 1) * NX + j, along_y(d))
            to_partner(h, 0, at_x(j))
            two[j - 1].wait_recv()
            for d in range(1, NX):
                over_x[d][j] = send(h, 1, at_y(j), second_recv, 12 + (d - 1) * NY + j, along_x(d))
            to_partner(h, 1, at_y(j))
    for h in range(2):
        one, two, over_y, over_x = over[h]
        for j in range(4):
            for d in range(1, 4):
                over_y[d][j].wait_recv()
                to_partner(h, 0, at_both(d, j))
                over_x[d][j].wait_recv()
                to_partner(h, 1, at_both(j, d))
    some = out_ref.at[:, pl.ds(0, W // 2)]
    remote(some, some, gather_send, pair_recv, partner).wait_recv()
    some = out_ref.at[:, pl.ds(0, GATHER_COPIES * 64)]
    remote(some, some, gather_send, pair_recv, partner).wait_send()
    for copy in rows_moved + deep_moved + [near_names, far_names]:
        copy.wait_send()


def step(gather, inverse, common, chosen, counts, momentum, gradient, params):
    vmem = pl.BlockSpec(memory_space=pltpu.VMEM)
    outside = pl.BlockSpec(memory_space=pltpu.HBM)
    dma = pltpu.SemaphoreType.DMA
    return pl.pallas_call(
        step_kernel,
        out_shape=(pltpu.VMEM((CH, W), f32), pltpu.VMEM((CH, W), f32)),
        in_specs=[outside] * 8,
        out_specs=(vmem, vmem),
        scratch_shapes=[
            pltpu.VMEM((128, 3 * CH), bf16),
            pltpu.VMEM((256, 128), bf16),
            pltpu.VMEM((Q, SPANS), jnp.int32),
            pltpu.VMEM((S, SPANS), jnp.int32),
            pltpu.VMEM((1, SPANS), jnp.int32),
            dma((5,)),
            pltpu.VMEM((CH, W), f32),
            pltpu.VMEM((CH, W), f32),
            pltpu.VMEM((SPANS * Q, 128), f32),
            pltpu.VMEM((SPANS * S, 128), f32),
            pltpu.VMEM((SPANS * Q, 3 * CH), bf16),
            pltpu.VMEM((SPANS * S, 3 * CH), f32),
            pltpu.VMEM((4 * S, W), f32),
            pltpu.VMEM((Q, W), f32),
            pltpu.VMEM((2, PLANE, Q, 128), f32),
            pltpu.VMEM((2, NZ, NX, Q, 128), f32),
            pltpu.VMEM((NX, Q, SPANS), f32),
            pltpu.VMEM((NZ, Q, 128), f32),
            pltpu.VMEM((2, CH, 128), f32),
            dma((TILES,)), dma((TILES,)), dma((2,)), dma((2,)), dma((2,)), dma((2,)), dma((2,)), dma((2,)), dma((2,)),
            dma, dma((2, 6)), dma((2, 24)), dma,
        ],
        compiler_params=pltpu.CompilerParams(collective_id=0, has_side_effects=True, vmem_limit_bytes=VMEM_GRANT),
        name="step",
    )(gather, inverse, common, chosen, counts, momentum, gradient, params)


def deliver_kernel(first_ref, second_ref, first_out, second_out, sems):
    copies = []
    for t in range(TILES):
        for i, (src, dst) in enumerate([(first_ref, first_out), (second_ref, second_out)]):
            at = pl.ds(t * TILE, TILE)
            copies.append(pltpu.make_async_copy(src.at[:, at], dst.at[:, at], sems.at[i, t]))
    for copy in copies:
        copy.start()
    for copy in copies:
        copy.wait()


def deliver(first, second):
    vmem = pl.BlockSpec(memory_space=pltpu.VMEM)
    outside = pl.BlockSpec(memory_space=pltpu.HBM)
    shape = jax.ShapeDtypeStruct((CH, W), f32)
    return pl.pallas_call(
        deliver_kernel,
        out_shape=(shape, shape),
        in_specs=[vmem, vmem],
        out_specs=(outside, outside),
        scratch_shapes=[pltpu.SemaphoreType.DMA((2, TILES))],
        compiler_params=pltpu.CompilerParams(vmem_limit_bytes=1 << 20),
        name="deliver",
    )(first, second)


def body(params, momentum, gradient, chosen_rows, live_counts, common_rows):
    high, low = table_parts()
    gather = np.concatenate([high.T, low.T, high.T], axis=1)
    gather = jnp.asarray(np.concatenate([gather, np.zeros_like(gather)], axis=0))
    inverse = jnp.asarray(np.concatenate([np.kron(np.eye(2, dtype=bf16), part) for part in (high, low)], axis=0))
    new_params, residual = step(
        gather, inverse, common_rows[0].T, chosen_rows[0, 0].T, live_counts[0], momentum[0, 0], gradient[0, 0], params
    )
    new_params, residual = deliver(new_params, residual)
    return (new_params, residual[None, None])


def solution(mesh):
    placed = (
        P(),
        P("row", "col", None, None),
        P("row", "col", None, None),
        P("row", "col", None, None),
        P("row", "col", None),
        P("col", None, None),
    )
    return jax.shard_map(
        body,
        mesh=mesh,
        in_specs=placed,
        out_specs=(P(), P("row", "col", None, None)),
        check_vma=False,
    )
```

```python
import math

import jax
import jax.numpy as jnp
import numpy as np
from jax import lax
from jax.experimental import pallas as pl
from jax.experimental.pallas import tpu as pltpu
from jax.sharding import PartitionSpec as P

CH = 64
W = 8192
SPANS = 128
S = 4
Q = 8
NY, NCORE, NZ, NX = 4, 2, 8, 4
PLANE = NY * NCORE * NX
OWN = W // PLANE
TILE = 1024
TILES = W // TILE
SUB = 256
GATHER_COPIES = 2 * (2 * 3 + 2 * 12 + 2 * 16)
EARLY, LATE = (0, 1, 2), (3, 6, 4, 5, 7)
VMEM_GRANT = 67043328 - 2 * 4 * CH * W - 4096

decay_rate = 0.9
step_size = 0.1
MESH = pl.DeviceIdType.MESH
f32 = jnp.float32
bf16 = jnp.bfloat16


def dct_table(order):
    freq = np.arange(order)[:, None]
    place = np.arange(order)[None, :]
    matrix = math.sqrt(2.0 / order) * np.cos(math.pi * (2.0 * place + 1.0) * freq / (2.0 * order))
    return np.where(freq == 0, matrix * math.sqrt(0.5), matrix).astype(np.float32)


def table_parts():
    back = dct_table(CH).T
    high = back.astype(bf16)
    return high, (back - high.astype(np.float32)).astype(bf16)


def steps_by_distance():
    steps = [(dy, dk, dx) for dy in range(NY) for dk in range(NCORE) for dx in range(NX)][1:]
    return sorted(steps, key=lambda s: -(min(s[0], NY - s[0]) + min(s[2], NX - s[2])))


def two_parts(value):
    high = value.astype(bf16)
    return high, (value - high.astype(f32)).astype(bf16)


def step_kernel(
    gather_hbm, inverse_hbm, common_hbm, chosen_hbm, counts_hbm, moment_ref, grad_ref, params_ref,
    out_ref, residual_ref,
    gather_ref, inverse_ref, common_ref, chosen_ref, counts_ref, small_sem,
    decayed, grads, hot_wanted, hot_chosen, wanted_rows, chosen_rows, chosen_values, own, parts, values, near, names, mine,
    moment_sem, grad_sem, param_sem, name_send, name_recv, row_send, row_recv, deep_send, deep_recv,
    gather_send, first_recv, second_recv, pair_recv,
):
    r = lax.axis_index("row")
    c = lax.axis_index("col")
    z, x = c // NX, lax.rem(c, NX)
    y, core = r // NCORE, lax.rem(r, NCORE)
    m = r * NX + x

    def in_plane(index):
        return (index // NX, z * NX + lax.rem(index, NX))

    def shifted(dy, dk, dx):
        row = lax.rem(y + dy, NY) * NCORE + lax.rem(core + dk, NCORE)
        return row * NX + lax.rem(x + dx, NX)

    def along_x(d):
        return (r, z * NX + lax.rem(x + d, NX))

    def along_y(d):
        return (lax.rem(y + d, NY) * NCORE + core, c)

    def along_z(d):
        return (r, lax.rem(z + d, NZ) * NX + x)

    def lanes(index, size):
        return pl.ds(pl.multiple_of(index * size, size), size)

    def half_lanes(index, h):
        return pl.ds(pl.multiple_of(h * (W // 2) + 128 * index, 128), 128)

    def remote(src, dst, send, recv, device):
        return pltpu.make_async_remote_copy(
            src_ref=src, dst_ref=dst, send_sem=send, recv_sem=recv, device_id=device, device_id_type=MESH
        )

    def moment_in(t):
        return pltpu.make_async_copy(moment_ref.at[:, lanes(t, TILE)], decayed.at[:, lanes(t, TILE)], moment_sem.at[t])

    def grad_in(t):
        return pltpu.make_async_copy(grad_ref.at[:, lanes(t, TILE)], grads.at[:, lanes(t, TILE)], grad_sem.at[t])

    barrier = pltpu.get_barrier_semaphore()

    def greet_deep(d, carry):
        pl.semaphore_signal(barrier, inc=1, device_id=along_z(d), device_id_type=MESH)
        return carry

    for step in steps_by_distance():
        there = shifted(*step)
        pl.semaphore_signal(barrier, inc=1, device_id=in_plane(there), device_id_type=MESH)

    lax.fori_loop(1, NZ, greet_deep, 0)
    smalls = [
        pltpu.make_async_copy(src, dst, small_sem.at[i])
        for i, (src, dst) in enumerate(
            [
                (chosen_hbm, chosen_ref),
                (counts_hbm, counts_ref),
                (common_hbm, common_ref),
                (gather_hbm, gather_ref),
                (inverse_hbm, inverse_ref),
            ]
        )
    ]
    for copy in smalls:
        copy.start()
    for t in range(TILES // 2):
        moment_in(t).start()
        grad_in(t).start()
    params_in = [
        pltpu.make_async_copy(params_ref.at[:, half_lanes(m, h)], mine.at[h], param_sem.at[h]) for h in range(2)
    ]
    for copy in params_in:
        copy.start()
    for copy in smalls:
        copy.wait()
    common = common_ref[...]
    place = lax.broadcasted_iota(jnp.int32, (S, SPANS), 0)
    chosen = jnp.where(place < counts_ref[...], chosen_ref[...], -1)
    found = common == chosen[0:1]
    for s in range(1, S):
        found = found | (common == chosen[s : s + 1])
    wanted = jnp.where(found, common, -1)
    freq = lax.broadcasted_iota(jnp.int32, (128, SPANS), 0)
    for q in range(Q):
        hot_wanted[pl.ds(q, SPANS, stride=Q), :] = jnp.where(wanted[q : q + 1] == freq, 1.0, 0.0).T
    for s in range(S):
        hot_chosen[pl.ds(s, SPANS, stride=S), :] = jnp.where(chosen[s : s + 1] == freq, 1.0, 0.0).T
    wanted_rows[...] = jnp.dot(
        hot_wanted[...].astype(bf16), gather_ref[...], preferred_element_type=f32
    ).astype(bf16)
    chosen_rows[...] = jnp.dot(hot_chosen[...].astype(bf16), gather_ref[...], preferred_element_type=f32)
    near[x] = common.astype(f32)
    left_lane = lax.broadcasted_iota(jnp.int32, (8, 128), 1) < CH

    def local_sums(t, carry):
        moment_in(t).wait()
        grad_in(t).wait()

        @pl.when(t < TILES // 2)
        def _():
            moment_in(t + TILES // 2).start()
            grad_in(t + TILES // 2).start()

        for i in range(TILE // SUB):
            at = pl.ds(pl.multiple_of(t * TILE + i * SUB, SUB), SUB)
            field = decay_rate * decayed[:, at] + grads[:, at]
            decayed[:, at] = field
            high, low = two_parts(field)
            step = t * (TILE // SUB) + i
            left = jnp.concatenate(
                [
                    wanted_rows[pl.ds(pl.multiple_of(step * 4 * Q, 4 * Q), 4 * Q), :],
                    chosen_rows[pl.ds(pl.multiple_of(step * 4 * S, 4 * S), 4 * S), :].astype(bf16),
                ],
                axis=0,
            )
            picked = jnp.dot(left, jnp.concatenate([high, high, low], axis=0), preferred_element_type=f32)
            for h in range(2):
                part = picked[16 * h : 16 * h + 16, 128 * h : 128 * h + 128]
                own[:, pl.ds(pl.multiple_of(t * TILE + i * SUB + 128 * h, 128), 128)] = jnp.where(
                    left_lane, part[:8], part[8:]
                )
            chosen_values[:, at] = picked[4 * Q :]
        return carry

    for h in range(2):
        lax.fori_loop(h * (TILES // 2), (h + 1) * (TILES // 2), local_sums, 0)
        if h == 0:
            pl.semaphore_wait(barrier, PLANE - 1 + NZ - 1)
            for d in range(1, NX):
                remote(near.at[x], near.at[x], name_send.at[0], name_recv.at[0], along_x(d)).start()

        for step in steps_by_distance():
            there = shifted(*step)
            remote(
                own.at[:, half_lanes(there, h)], parts.at[h, m], row_send.at[h], row_recv.at[h], in_plane(there)
            ).start()
        parts[h, m] = own[:, half_lanes(m, h)]
    some = near.at[pl.ds(0, NX - 1)]
    near_names = remote(some, some, name_send.at[0], name_recv.at[0], along_x(1))
    near_names.wait_recv()
    lane = lax.broadcasted_iota(jnp.int32, (128, 128), 1)
    block = lax.broadcasted_iota(jnp.int32, (128, 128), 0)
    mine_of = m * 2 + lax.rem(lane, 2) + (SPANS // 2) * lax.rem(lane // 2, 2)
    listed = jnp.zeros((Q, 128), f32)
    for group in range(NX):
        pick = jnp.where((block == mine_of) & (lane // 4 == group), 1.0, 0.0).astype(bf16)
        listed = listed + jnp.dot(near[group].astype(bf16), pick, preferred_element_type=f32)
    names[z] = listed

    def send_names(d, carry):
        remote(names.at[z], names.at[z], name_send.at[1], name_recv.at[1], along_z(d)).start()
        return carry

    lax.fori_loop(1, NZ, send_names, 0)

    same = lax.broadcasted_iota(jnp.int32, (4 * S, SUB), 1) // CH == lax.broadcasted_iota(jnp.int32, (4 * S, SUB), 0) // S

    def residuals(t, carry):
        for i in range(TILE // SUB):
            at = pl.ds(pl.multiple_of(t * TILE + i * SUB, SUB), SUB)
            step = t * (TILE // SUB) + i
            rows = chosen_rows[pl.ds(pl.multiple_of(step * 4 * S, 4 * S), 4 * S), :]
            back = jnp.concatenate([rows[:, :CH], rows[:, :CH], rows[:, CH : 2 * CH]], axis=0).T.astype(bf16)
            high, low = two_parts(jnp.where(same, chosen_values[:, at], 0.0))
            sent = jnp.dot(back, jnp.concatenate([high, low, high], axis=0), preferred_element_type=f32)
            residual_ref[:, at] = decayed[:, at] - sent
        return carry

    lax.fori_loop(0, TILES, residuals, 0)

    def send_values(h, deep):
        @pl.when(z != deep)
        def _():
            remote(
                values.at[h, z], values.at[h, z], deep_send.at[h], deep_recv.at[h], (r, deep * NX + x)
            ).start()

    rows_moved = []
    for h in range(2):
        some = parts.at[h, pl.ds(0, PLANE - 1)]
        moved = remote(some, some, row_send.at[h], row_recv.at[h], along_x(1))
        moved.wait_recv()
        rows_moved.append(moved)
        for group in range(NX):
            total = parts[h, group]
            for other in range(1, NY * NCORE):
                total = total + parts[h, other * NX + group]
            values[h, z, group] = total
        for deep in EARLY:
            send_values(h, deep)
    for h in range(2):
        for deep in LATE:
            send_values(h, deep)

    some = names.at[pl.ds(0, NZ - 1)]
    far_names = remote(some, some, name_send.at[1], name_recv.at[1], along_z(1))
    far_names.wait_recv()
    listed = names[...].reshape(NZ * Q, 128).astype(bf16)
    wide_freq = lax.rem(lax.broadcasted_iota(jnp.int32, (NZ * NX * Q, 128), 1), CH).astype(f32)
    spreads = []
    for h in range(2):
        found_names = []
        for group in range(NX):
            pick = jnp.where(block == 4 * group + 2 * h + lane // CH, 1.0, 0.0).astype(bf16)
            found_names.append(jnp.dot(listed, pick, preferred_element_type=f32).reshape(NZ, Q, 128))
        spread_names = jnp.stack(found_names, axis=1).reshape(NZ * NX * Q, 128)
        hot = jnp.where(spread_names == wide_freq, 1.0, 0.0).T.astype(bf16)
        spreads.append(jnp.dot(inverse_ref[...], hot, preferred_element_type=f32).astype(bf16))
    for copy in params_in:
        copy.wait()
    left = lax.broadcasted_iota(jnp.int32, (CH, 128), 1) < CH

    def go(copy):
        copy.start()
        return copy

    def place_of(h, rows, index):
        return out_ref.at[pl.ds(32 * rows, 32), half_lanes(index, h)]

    def send(h, rows, index, sems, slot, device):
        at = place_of(h, rows, index)
        return go(remote(at, at, gather_send, sems.at[h, slot], device))

    partner = (y * NCORE + (1 - core), c)

    def to_partner(h, rows, index):
        at = place_of(h, rows, index)
        go(remote(at, at, gather_send, pair_recv, partner))

    def at_x(d):
        return r * NX + lax.rem(x + NX - d, NX)

    def at_y(d):
        return (lax.rem(y + NY - d, NY) * NCORE + core) * NX + x

    def at_both(dy, dx):
        return (lax.rem(y + NY - dy, NY) * NCORE + core) * NX + lax.rem(x + NX - dx, NX)

    deep_moved = []
    over = []
    for h in range(2):
        some = values.at[h, pl.ds(0, NZ - 1)]
        moved = remote(some, some, deep_send.at[h], deep_recv.at[h], along_z(1))
        moved.wait_recv()
        deep_moved.append(moved)
        high, low = two_parts(values[h].reshape(NZ * NX * Q, 128))
        both = jnp.dot(spreads[h], high, preferred_element_type=f32)
        both = both[:128] + both[128:] + jnp.dot(spreads[h][:128], low, preferred_element_type=f32)
        update = jnp.where(left, both[:CH], both[CH:])
        out_ref[:, half_lanes(m, h)] = mine[h] - step_size * update
        one, two = [None] * 3, [None] * 3
        for d in (2, 1, 3):
            one[d - 1] = send(h, 0, m, first_recv, d - 1, along_x(d))
            two[d - 1] = send(h, 1, m, first_recv, 2 + d, along_y(d))
        over_y = [[None] * NX for _ in range(NY)]
        over_x = [[None] * NY for _ in range(NX)]
        for d in (2, 1, 3):
            over_y[d][0] = send(h, 0, m, second_recv, (d - 1) * NX, along_y(d))
        for d in (2, 1, 3):
            over_x[d][0] = send(h, 1, m, second_recv, 12 + (d - 1) * NY, along_x(d))
        to_partner(h, 0, m)
        to_partner(h, 1, m)
        over.append((one, two, over_y, over_x))
    for h in range(2):
        one, two, over_y, over_x = over[h]
        for j in (1, 3, 2):
            one[j - 1].wait_recv()
            for d in (2, 1, 3):
                over_y[d][j] = send(h, 0, at_x(j), second_recv, (d - 1) * NX + j, along_y(d))
            to_partner(h, 0, at_x(j))
            two[j - 1].wait_recv()
            for d in (2, 1, 3):
                over_x[d][j] = send(h, 1, at_y(j), second_recv, 12 + (d - 1) * NY + j, along_x(d))
            to_partner(h, 1, at_y(j))
    for h in range(2):
        one, two, over_y, over_x = over[h]
        for j in (0, 1, 3, 2):
            for d in (1, 3, 2):
                over_y[d][j].wait_recv()
                to_partner(h, 0, at_both(d, j))
                over_x[d][j].wait_recv()
                to_partner(h, 1, at_both(j, d))
    some = out_ref.at[:, pl.ds(0, W // 2)]
    remote(some, some, gather_send, pair_recv, partner).wait_recv()
    some = out_ref.at[:, pl.ds(0, GATHER_COPIES * 64)]
    remote(some, some, gather_send, pair_recv, partner).wait_send()
    for copy in rows_moved + deep_moved + [near_names, far_names]:
        copy.wait_send()


def step(gather, inverse, common, chosen, counts, momentum, gradient, params):
    vmem = pl.BlockSpec(memory_space=pltpu.VMEM)
    outside = pl.BlockSpec(memory_space=pltpu.HBM)
    dma = pltpu.SemaphoreType.DMA
    return pl.pallas_call(
        step_kernel,
        out_shape=(pltpu.VMEM((CH, W), f32), pltpu.VMEM((CH, W), f32)),
        in_specs=[outside] * 8,
        out_specs=(vmem, vmem),
        scratch_shapes=[
            pltpu.VMEM((128, 3 * CH), bf16),
            pltpu.VMEM((256, 128), bf16),
            pltpu.VMEM((Q, SPANS), jnp.int32),
            pltpu.VMEM((S, SPANS), jnp.int32),
            pltpu.VMEM((1, SPANS), jnp.int32),
            dma((5,)),
            pltpu.VMEM((CH, W), f32),
            pltpu.VMEM((CH, W), f32),
            pltpu.VMEM((SPANS * Q, 128), f32),
            pltpu.VMEM((SPANS * S, 128), f32),
            pltpu.VMEM((SPANS * Q, 3 * CH), bf16),
            pltpu.VMEM((SPANS * S, 3 * CH), f32),
            pltpu.VMEM((4 * S, W), f32),
            pltpu.VMEM((Q, W), f32),
            pltpu.VMEM((2, PLANE, Q, 128), f32),
            pltpu.VMEM((2, NZ, NX, Q, 128), f32),
            pltpu.VMEM((NX, Q, SPANS), f32),
            pltpu.VMEM((NZ, Q, 128), f32),
            pltpu.VMEM((2, CH, 128), f32),
            dma((TILES,)), dma((TILES,)), dma((2,)), dma((2,)), dma((2,)), dma((2,)), dma((2,)), dma((2,)), dma((2,)),
            dma, dma((2, 6)), dma((2, 24)), dma,
        ],
        compiler_params=pltpu.CompilerParams(collective_id=0, has_side_effects=True, vmem_limit_bytes=VMEM_GRANT),
        name="step",
    )(gather, inverse, common, chosen, counts, momentum, gradient, params)


def deliver_kernel(first_ref, second_ref, first_out, second_out, sems):
    copies = []
    for t in range(TILES):
        for i, (src, dst) in enumerate([(first_ref, first_out), (second_ref, second_out)]):
            at = pl.ds(t * TILE, TILE)
            copies.append(pltpu.make_async_copy(src.at[:, at], dst.at[:, at], sems.at[i, t]))
    for copy in copies:
        copy.start()
    for copy in copies:
        copy.wait()


def deliver(first, second):
    vmem = pl.BlockSpec(memory_space=pltpu.VMEM)
    outside = pl.BlockSpec(memory_space=pltpu.HBM)
    shape = jax.ShapeDtypeStruct((CH, W), f32)
    return pl.pallas_call(
        deliver_kernel,
        out_shape=(shape, shape),
        in_specs=[vmem, vmem],
        out_specs=(outside, outside),
        scratch_shapes=[pltpu.SemaphoreType.DMA((2, TILES))],
        compiler_params=pltpu.CompilerParams(vmem_limit_bytes=1 << 20),
        name="deliver",
    )(first, second)


def body(params, momentum, gradient, chosen_rows, live_counts, common_rows):
    high, low = table_parts()
    gather = np.concatenate([high.T, low.T, high.T], axis=1)
    gather = jnp.asarray(np.concatenate([gather, np.zeros_like(gather)], axis=0))
    inverse = jnp.asarray(np.concatenate([np.kron(np.eye(2, dtype=bf16), part) for part in (high, low)], axis=0))
    new_params, residual = step(
        gather, inverse, common_rows[0].T, chosen_rows[0, 0].T, live_counts[0], momentum[0, 0], gradient[0, 0], params
    )
    new_params, residual = deliver(new_params, residual)
    return (new_params, residual[None, None])


def solution(mesh):
    placed = (
        P(),
        P("row", "col", None, None),
        P("row", "col", None, None),
        P("row", "col", None, None),
        P("row", "col", None),
        P("col", None, None),
    )
    return jax.shard_map(
        body,
        mesh=mesh,
        in_specs=placed,
        out_specs=(P(), P("row", "col", None, None)),
        check_vma=False,
    )
```

```python
import math

import jax
import jax.numpy as jnp
import numpy as np
from jax import lax
from jax.experimental import pallas as pl
from jax.experimental.pallas import tpu as pltpu
from jax.sharding import PartitionSpec as P

CH = 64
W = 8192
SPANS = 128
S = 4
Q = 8
NY, NCORE, NZ, NX = 4, 2, 8, 4
PLANE = NY * NCORE * NX
OWN = W // PLANE
TILE = 1024
TILES = W // TILE
SUB = 256
FIRST = (0, 1, 3, 2)
GATHER_COPIES = 2 * (2 * 3 + 2 * 12 + 2 * 16)
EARLY, LATE = (0, 1, 2), (3, 6, 4, 5, 7)
VMEM_GRANT = 67043328 - 2 * 4 * CH * W - 4096

decay_rate = 0.9
step_size = 0.1
MESH = pl.DeviceIdType.MESH
f32 = jnp.float32
bf16 = jnp.bfloat16


def dct_table(order):
    freq = np.arange(order)[:, None]
    place = np.arange(order)[None, :]
    matrix = math.sqrt(2.0 / order) * np.cos(math.pi * (2.0 * place + 1.0) * freq / (2.0 * order))
    return np.where(freq == 0, matrix * math.sqrt(0.5), matrix).astype(np.float32)


def table_parts():
    back = dct_table(CH).T
    high = back.astype(bf16)
    return high, (back - high.astype(np.float32)).astype(bf16)


def steps_by_distance():
    steps = [(dy, dk, dx) for dy in range(NY) for dk in range(NCORE) for dx in range(NX)][1:]
    return sorted(steps, key=lambda s: -(min(s[0], NY - s[0]) + min(s[2], NX - s[2])))


def two_parts(value):
    high = value.astype(bf16)
    return high, (value - high.astype(f32)).astype(bf16)


def step_kernel(
    gather_hbm, inverse_hbm, common_hbm, chosen_hbm, counts_hbm, moment_ref, grad_ref, params_ref,
    out_ref, residual_ref,
    gather_ref, inverse_ref, common_ref, chosen_ref, counts_ref, small_sem,
    decayed, grads, hot_wanted, hot_chosen, wanted_rows, chosen_rows, chosen_values, own, parts, values, near, names, mine,
    moment_sem, grad_sem, param_sem, name_send, name_recv, row_send, row_recv, deep_send, deep_recv,
    gather_send, first_recv, second_recv, pair_recv,
):
    r = lax.axis_index("row")
    c = lax.axis_index("col")
    z, x = c // NX, lax.rem(c, NX)
    y, core = r // NCORE, lax.rem(r, NCORE)
    m = r * NX + x

    def in_plane(index):
        return (index // NX, z * NX + lax.rem(index, NX))

    def shifted(dy, dk, dx):
        row = lax.rem(y + dy, NY) * NCORE + lax.rem(core + dk, NCORE)
        return row * NX + lax.rem(x + dx, NX)

    def along_x(d):
        return (r, z * NX + lax.rem(x + d, NX))

    def along_y(d):
        return (lax.rem(y + d, NY) * NCORE + core, c)

    def along_z(d):
        return (r, lax.rem(z + d, NZ) * NX + x)

    def lanes(index, size):
        return pl.ds(pl.multiple_of(index * size, size), size)

    def half_lanes(index, h):
        return pl.ds(pl.multiple_of(h * (W // 2) + 128 * index, 128), 128)

    def remote(src, dst, send, recv, device):
        return pltpu.make_async_remote_copy(
            src_ref=src, dst_ref=dst, send_sem=send, recv_sem=recv, device_id=device, device_id_type=MESH
        )

    def moment_in(t):
        return pltpu.make_async_copy(moment_ref.at[:, lanes(t, TILE)], decayed.at[:, lanes(t, TILE)], moment_sem.at[t])

    def grad_in(t):
        return pltpu.make_async_copy(grad_ref.at[:, lanes(t, TILE)], grads.at[:, lanes(t, TILE)], grad_sem.at[t])

    barrier = pltpu.get_barrier_semaphore()

    def greet_deep(d, carry):
        pl.semaphore_signal(barrier, inc=1, device_id=along_z(d), device_id_type=MESH)
        return carry

    for step in steps_by_distance():
        there = shifted(*step)
        pl.semaphore_signal(barrier, inc=1, device_id=in_plane(there), device_id_type=MESH)

    lax.fori_loop(1, NZ, greet_deep, 0)
    smalls = [
        pltpu.make_async_copy(src, dst, small_sem.at[i])
        for i, (src, dst) in enumerate(
            [
                (chosen_hbm, chosen_ref),
                (counts_hbm, counts_ref),
                (common_hbm, common_ref),
                (gather_hbm, gather_ref),
                (inverse_hbm, inverse_ref),
            ]
        )
    ]
    for copy in smalls:
        copy.start()
    for t in range(TILES // 2):
        moment_in(t).start()
        grad_in(t).start()
    params_in = [
        pltpu.make_async_copy(params_ref.at[:, half_lanes(m, h)], mine.at[h], param_sem.at[h]) for h in range(2)
    ]
    for copy in params_in:
        copy.start()
    for copy in smalls:
        copy.wait()
    common = common_ref[...]
    place = lax.broadcasted_iota(jnp.int32, (S, SPANS), 0)
    chosen = jnp.where(place < counts_ref[...], chosen_ref[...], -1)
    found = common == chosen[0:1]
    for s in range(1, S):
        found = found | (common == chosen[s : s + 1])
    wanted = jnp.where(found, common, -1)
    freq = lax.broadcasted_iota(jnp.int32, (128, SPANS), 0)
    for q in range(Q):
        hot_wanted[pl.ds(q, SPANS, stride=Q), :] = jnp.where(wanted[q : q + 1] == freq, 1.0, 0.0).T
    for s in range(S):
        hot_chosen[pl.ds(s, SPANS, stride=S), :] = jnp.where(chosen[s : s + 1] == freq, 1.0, 0.0).T
    wanted_rows[...] = jnp.dot(
        hot_wanted[...].astype(bf16), gather_ref[...], preferred_element_type=f32
    ).astype(bf16)
    chosen_rows[...] = jnp.dot(hot_chosen[...].astype(bf16), gather_ref[...], preferred_element_type=f32)
    near[x] = common.astype(f32)
    left_lane = lax.broadcasted_iota(jnp.int32, (8, 128), 1) < CH

    def local_sums(t, carry):
        moment_in(t).wait()
        grad_in(t).wait()

        @pl.when(t < TILES // 2)
        def _():
            moment_in(t + TILES // 2).start()
            grad_in(t + TILES // 2).start()

        for i in range(TILE // SUB):
            at = pl.ds(pl.multiple_of(t * TILE + i * SUB, SUB), SUB)
            field = decay_rate * decayed[:, at] + grads[:, at]
            decayed[:, at] = field
            high, low = two_parts(field)
            step = t * (TILE // SUB) + i
            left = jnp.concatenate(
                [
                    wanted_rows[pl.ds(pl.multiple_of(step * 4 * Q, 4 * Q), 4 * Q), :],
                    chosen_rows[pl.ds(pl.multiple_of(step * 4 * S, 4 * S), 4 * S), :].astype(bf16),
                ],
                axis=0,
            )
            picked = jnp.dot(left, jnp.concatenate([high, high, low], axis=0), preferred_element_type=f32)
            for h in range(2):
                part = picked[16 * h : 16 * h + 16, 128 * h : 128 * h + 128]
                own[:, pl.ds(pl.multiple_of(t * TILE + i * SUB + 128 * h, 128), 128)] = jnp.where(
                    left_lane, part[:8], part[8:]
                )
            chosen_values[:, at] = picked[4 * Q :]
        return carry

    for h in range(2):
        lax.fori_loop(h * (TILES // 2), (h + 1) * (TILES // 2), local_sums, 0)
        if h == 0:
            pl.semaphore_wait(barrier, PLANE - 1 + NZ - 1)
            for d in range(1, NX):
                remote(near.at[x], near.at[x], name_send.at[0], name_recv.at[0], along_x(d)).start()

        for step in steps_by_distance():
            there = shifted(*step)
            remote(
                own.at[:, half_lanes(there, h)], parts.at[h, m], row_send.at[h], row_recv.at[h], in_plane(there)
            ).start()
        parts[h, m] = own[:, half_lanes(m, h)]
    some = near.at[pl.ds(0, NX - 1)]
    near_names = remote(some, some, name_send.at[0], name_recv.at[0], along_x(1))
    near_names.wait_recv()
    lane = lax.broadcasted_iota(jnp.int32, (128, 128), 1)
    block = lax.broadcasted_iota(jnp.int32, (128, 128), 0)
    mine_of = m * 2 + lax.rem(lane, 2) + (SPANS // 2) * lax.rem(lane // 2, 2)
    listed = jnp.zeros((Q, 128), f32)
    for group in range(NX):
        pick = jnp.where((block == mine_of) & (lane // 4 == group), 1.0, 0.0).astype(bf16)
        listed = listed + jnp.dot(near[group].astype(bf16), pick, preferred_element_type=f32)
    names[z] = listed

    def send_names(d, carry):
        remote(names.at[z], names.at[z], name_send.at[1], name_recv.at[1], along_z(d)).start()
        return carry

    lax.fori_loop(1, NZ, send_names, 0)

    same = lax.broadcasted_iota(jnp.int32, (4 * S, SUB), 1) // CH == lax.broadcasted_iota(jnp.int32, (4 * S, SUB), 0) // S

    def residuals(t, carry):
        for i in range(TILE // SUB):
            at = pl.ds(pl.multiple_of(t * TILE + i * SUB, SUB), SUB)
            step = t * (TILE // SUB) + i
            rows = chosen_rows[pl.ds(pl.multiple_of(step * 4 * S, 4 * S), 4 * S), :]
            back = jnp.concatenate([rows[:, :CH], rows[:, :CH], rows[:, CH : 2 * CH]], axis=0).T.astype(bf16)
            high, low = two_parts(jnp.where(same, chosen_values[:, at], 0.0))
            sent = jnp.dot(back, jnp.concatenate([high, low, high], axis=0), preferred_element_type=f32)
            residual_ref[:, at] = decayed[:, at] - sent
        return carry

    lax.fori_loop(0, TILES, residuals, 0)

    def send_values(h, deep):
        @pl.when(z != deep)
        def _():
            remote(
                values.at[h, z], values.at[h, z], deep_send.at[h], deep_recv.at[h], (r, deep * NX + x)
            ).start()

    rows_moved = []
    for h in range(2):
        some = parts.at[h, pl.ds(0, PLANE - 1)]
        moved = remote(some, some, row_send.at[h], row_recv.at[h], along_x(1))
        moved.wait_recv()
        rows_moved.append(moved)
        for group in range(NX):
            total = parts[h, group]
            for other in range(1, NY * NCORE):
                total = total + parts[h, other * NX + group]
            values[h, z, group] = total
        for deep in EARLY:
            send_values(h, deep)
    for h in range(2):
        for deep in LATE:
            send_values(h, deep)

    some = names.at[pl.ds(0, NZ - 1)]
    far_names = remote(some, some, name_send.at[1], name_recv.at[1], along_z(1))
    far_names.wait_recv()
    listed = names[...].reshape(NZ * Q, 128).astype(bf16)
    wide_freq = lax.rem(lax.broadcasted_iota(jnp.int32, (NZ * NX * Q, 128), 1), CH).astype(f32)
    spreads = []
    for h in range(2):
        found_names = []
        for group in range(NX):
            pick = jnp.where(block == 4 * group + 2 * h + lane // CH, 1.0, 0.0).astype(bf16)
            found_names.append(jnp.dot(listed, pick, preferred_element_type=f32).reshape(NZ, Q, 128))
        spread_names = jnp.stack(found_names, axis=1).reshape(NZ * NX * Q, 128)
        hot = jnp.where(spread_names == wide_freq, 1.0, 0.0).T.astype(bf16)
        spreads.append(jnp.dot(inverse_ref[...], hot, preferred_element_type=f32).astype(bf16))
    for copy in params_in:
        copy.wait()
    left = lax.broadcasted_iota(jnp.int32, (CH, 128), 1) < CH

    def go(copy):
        copy.start()
        return copy

    def place_of(h, rows, index):
        return out_ref.at[pl.ds(32 * rows, 32), half_lanes(index, h)]

    def send(h, rows, index, sem, device):
        at = place_of(h, rows, index)
        go(remote(at, at, gather_send, sem, device))

    def arrived(h, rows, index, sem):
        at = place_of(h, rows, index)
        remote(at, at, gather_send, sem, partner).wait_recv()

    def send_over_x(h, rows, index, sem_of):
        for there in FIRST:

            @pl.when(x != there)
            def _():
                send(h, rows, index, sem_of(lax.rem(there + NX - x, NX)), (r, z * NX + there))

    def send_over_y(h, rows, index, sem_of):
        for there in FIRST:

            @pl.when(y != there)
            def _():
                send(h, rows, index, sem_of(lax.rem(there + NY - y, NY)), (there * NCORE + core, c))

    partner = (y * NCORE + (1 - core), c)

    def to_partner(h, rows, index):
        at = place_of(h, rows, index)
        go(remote(at, at, gather_send, pair_recv, partner))

    def at_x(d):
        return r * NX + lax.rem(x + NX - d, NX)

    def at_y(d):
        return (lax.rem(y + NY - d, NY) * NCORE + core) * NX + x

    def at_both(dy, dx):
        return (lax.rem(y + NY - dy, NY) * NCORE + core) * NX + lax.rem(x + NX - dx, NX)

    deep_moved = []
    for h in range(2):
        some = values.at[h, pl.ds(0, NZ - 1)]
        moved = remote(some, some, deep_send.at[h], deep_recv.at[h], along_z(1))
        moved.wait_recv()
        deep_moved.append(moved)
        high, low = two_parts(values[h].reshape(NZ * NX * Q, 128))
        both = jnp.dot(spreads[h], high, preferred_element_type=f32)
        both = both[:128] + both[128:] + jnp.dot(spreads[h][:128], low, preferred_element_type=f32)
        update = jnp.where(left, both[:CH], both[CH:])
        out_ref[:, half_lanes(m, h)] = mine[h] - step_size * update
        send_over_x(h, 0, m, lambda d: first_recv.at[h, d - 1])
        send_over_y(h, 1, m, lambda d: first_recv.at[h, 2 + d])
        send_over_y(h, 0, m, lambda d: second_recv.at[h, (d - 1) * NX])
        send_over_x(h, 1, m, lambda d: second_recv.at[h, 12 + (d - 1) * NY])
        to_partner(h, 0, m)
        to_partner(h, 1, m)
    for h in range(2):
        for j in (1, 3, 2):
            arrived(h, 0, at_x(j), first_recv.at[h, j - 1])
            send_over_y(h, 0, at_x(j), lambda d: second_recv.at[h, (d - 1) * NX + j])
            to_partner(h, 0, at_x(j))
            arrived(h, 1, at_y(j), first_recv.at[h, 2 + j])
            send_over_x(h, 1, at_y(j), lambda d: second_recv.at[h, 12 + (d - 1) * NY + j])
            to_partner(h, 1, at_y(j))
    for h in range(2):
        for j in (0, 1, 3, 2):
            for d in (1, 3, 2):
                arrived(h, 0, at_both(d, j), second_recv.at[h, (d - 1) * NX + j])
                to_partner(h, 0, at_both(d, j))
                arrived(h, 1, at_both(j, d), second_recv.at[h, 12 + (d - 1) * NY + j])
                to_partner(h, 1, at_both(j, d))
    some = out_ref.at[:, pl.ds(0, W // 2)]
    remote(some, some, gather_send, pair_recv, partner).wait_recv()
    some = out_ref.at[:, pl.ds(0, GATHER_COPIES * 64)]
    remote(some, some, gather_send, pair_recv, partner).wait_send()
    for copy in rows_moved + deep_moved + [near_names, far_names]:
        copy.wait_send()


def step(gather, inverse, common, chosen, counts, momentum, gradient, params):
    vmem = pl.BlockSpec(memory_space=pltpu.VMEM)
    outside = pl.BlockSpec(memory_space=pltpu.HBM)
    dma = pltpu.SemaphoreType.DMA
    return pl.pallas_call(
        step_kernel,
        out_shape=(pltpu.VMEM((CH, W), f32), pltpu.VMEM((CH, W), f32)),
        in_specs=[outside] * 8,
        out_specs=(vmem, vmem),
        scratch_shapes=[
            pltpu.VMEM((128, 3 * CH), bf16),
            pltpu.VMEM((256, 128), bf16),
            pltpu.VMEM((Q, SPANS), jnp.int32),
            pltpu.VMEM((S, SPANS), jnp.int32),
            pltpu.VMEM((1, SPANS), jnp.int32),
            dma((5,)),
            pltpu.VMEM((CH, W), f32),
            pltpu.VMEM((CH, W), f32),
            pltpu.VMEM((SPANS * Q, 128), f32),
            pltpu.VMEM((SPANS * S, 128), f32),
            pltpu.VMEM((SPANS * Q, 3 * CH), bf16),
            pltpu.VMEM((SPANS * S, 3 * CH), f32),
            pltpu.VMEM((4 * S, W), f32),
            pltpu.VMEM((Q, W), f32),
            pltpu.VMEM((2, PLANE, Q, 128), f32),
            pltpu.VMEM((2, NZ, NX, Q, 128), f32),
            pltpu.VMEM((NX, Q, SPANS), f32),
            pltpu.VMEM((NZ, Q, 128), f32),
            pltpu.VMEM((2, CH, 128), f32),
            dma((TILES,)), dma((TILES,)), dma((2,)), dma((2,)), dma((2,)), dma((2,)), dma((2,)), dma((2,)), dma((2,)),
            dma, dma((2, 6)), dma((2, 24)), dma,
        ],
        compiler_params=pltpu.CompilerParams(collective_id=0, has_side_effects=True, vmem_limit_bytes=VMEM_GRANT),
        name="step",
    )(gather, inverse, common, chosen, counts, momentum, gradient, params)


def deliver_kernel(first_ref, second_ref, first_out, second_out, sems):
    copies = []
    for t in range(TILES):
        for i, (src, dst) in enumerate([(first_ref, first_out), (second_ref, second_out)]):
            at = pl.ds(t * TILE, TILE)
            copies.append(pltpu.make_async_copy(src.at[:, at], dst.at[:, at], sems.at[i, t]))
    for copy in copies:
        copy.start()
    for copy in copies:
        copy.wait()


def deliver(first, second):
    vmem = pl.BlockSpec(memory_space=pltpu.VMEM)
    outside = pl.BlockSpec(memory_space=pltpu.HBM)
    shape = jax.ShapeDtypeStruct((CH, W), f32)
    return pl.pallas_call(
        deliver_kernel,
        out_shape=(shape, shape),
        in_specs=[vmem, vmem],
        out_specs=(outside, outside),
        scratch_shapes=[pltpu.SemaphoreType.DMA((2, TILES))],
        compiler_params=pltpu.CompilerParams(vmem_limit_bytes=1 << 20),
        name="deliver",
    )(first, second)


def body(params, momentum, gradient, chosen_rows, live_counts, common_rows):
    high, low = table_parts()
    gather = np.concatenate([high.T, low.T, high.T], axis=1)
    gather = jnp.asarray(np.concatenate([gather, np.zeros_like(gather)], axis=0))
    inverse = jnp.asarray(np.concatenate([np.kron(np.eye(2, dtype=bf16), part) for part in (high, low)], axis=0))
    new_params, residual = step(
        gather, inverse, common_rows[0].T, chosen_rows[0, 0].T, live_counts[0], momentum[0, 0], gradient[0, 0], params
    )
    new_params, residual = deliver(new_params, residual)
    return (new_params, residual[None, None])


def solution(mesh):
    placed = (
        P(),
        P("row", "col", None, None),
        P("row", "col", None, None),
        P("row", "col", None, None),
        P("row", "col", None),
        P("col", None, None),
    )
    return jax.shard_map(
        body,
        mesh=mesh,
        in_specs=placed,
        out_specs=(P(), P("row", "col", None, None)),
        check_vma=False,
    )
```
